32 devices in a mesh: grp: 2 (over y), seq: 4 (over z), sub: 2 (over x), rep: 2 (over core).
Axes of the slice: x: 2, y: 2, z: 4, core: 2. Of those that a mesh axis runs over, the one named last changes fastest.
Arguments:
- inputs: bfloat16 [16, 4096, 4096], P(('grp', 'rep'), ('seq', 'sub')), parts along dimension 0, may hold values from -6 to 6
- out_grads: bfloat16 [16, 4096, 4096], P(('grp', 'rep'), ('seq', 'sub')), parts along dimension 0, may hold values from -6 to 6
- doc_lengths: int32 [16], P(('grp', 'rep')), parts along dimension 0, may hold values from 512 to 4096, as said below
- in_proj: bfloat16 [4096, 256], replicated, may hold values from -0.09375 to 0.09375
- out_proj: bfloat16 [4096, 256], replicated, may hold values from -0.09375 to 0.09375
- in_factor: float32 [256, 256], replicated, may hold values from -0.25 to 2.25, as said below
- out_factor: float32 [256, 256], replicated, may hold values from -0.25 to 2.25, as said below
- index_rows: bfloat16 [4096, 65536], P('grp', ('seq', 'sub', 'rep')), parts along dimension 0, may hold values from -0.00048828125 to 0.00048828125
Outputs:
- scores: float32 [4096, 8], P(('grp', 'seq', 'sub', 'rep')), parts along dimension 0
The draws below stay inside these ranges and needn't reach their ends.
There are 2 independent parts, one for each index of `grp`. The reference program is written for one: setup_inputs(seed, part) draws one part's arguments, and reference() takes and returns one part's arrays. A program takes and returns all parts, laid end to end along the dimension named above; an argument that names none is the same for every part. Nothing has to cross between parts.
Inputs may be any that keep to these rules, and one draw needn't show every extreme that they name: `doc_lengths`: positions from a document's length on are padding. `in_factor`: symmetric. `out_factor`: symmetric.
All inputs are finite; a program needn't handle non-finite values.
Results may differ from the reference program's by a relative error of at most 0.005.
Values may be sent and summed in bfloat16 or wider, within the bound.
No kernel may reach another device: no remote copies, remote signals or barrier semaphores. Data moves between devices by JAX's collectives and lax.ppermute only.
A program may use at most 128 MiB of HBM per device.

```python
import jax
import jax.numpy as jnp
from jax import lax

D = 4096
R = 256
LEN = 4096
DOCS = 8
ROWS = 2048
F = 65536


def factor_matrix(key):
    key_diag, key_noise = jax.random.split(key)
    diagonal_part = jax.random.uniform(key_diag, (R,), jnp.float32, 0.5, 2.0)
    noise = jax.random.normal(key_noise, (R, R), jnp.float32)
    noise = jnp.clip(noise, -4.0, 4.0)
    symmetric = (noise + noise.T) * (0.25 / jnp.sqrt(jnp.float32(R)))
    return (jnp.diag(diagonal_part) + symmetric).astype(jnp.float32)


def draw_in_factor(key, part):
    return factor_matrix(jax.random.fold_in(key, 11))


def draw_out_factor(key, part):
    return factor_matrix(jax.random.fold_in(key, 23))


def draw_doc_lengths(key, part):
    key_len, key_perm = jax.random.split(jax.random.fold_in(key, 37))
    lengths = jax.random.randint(key_len, (DOCS,), LEN // 8, LEN + 1).astype(jnp.int32)
    order = jax.random.permutation(key_perm, DOCS)
    lengths = lengths.at[order[0]].set(LEN)
    lengths = lengths.at[order[1]].set(LEN // 8)
    return lengths.astype(jnp.int32)


def raised(drawn, stream_key, source, target, parts, factor):
    def block_of(position):
        return (jnp.arange(drawn.shape[position]) // (drawn.shape[position] // parts)).reshape((-1,) + (1,) * (drawn.ndim - 1 - position))

    first = jax.random.permutation(stream_key, parts)[block_of(target)]
    other_side = (block_of(target) + parts // 2) % parts
    return jnp.where((block_of(source) == first) | (block_of(source) == other_side), factor * drawn, drawn)


def level_of(own_key, dims, cuts, low, largest):
    gain = 1.0
    for position, parts in cuts:
        draws = jax.random.uniform(jax.random.fold_in(jax.random.fold_in(own_key, 6), position), (parts,), jnp.float32, low / len(cuts), largest / len(cuts))
        gain = gain * jnp.repeat(jnp.exp(draws), dims[position] // parts).reshape((-1,) + (1,) * (len(dims) - 1 - position))
    return gain


def centred(key, dims, deviation, bound, shards=(), kind=jnp.bfloat16):
    array = jax.random.normal(key, dims, jnp.float32) * deviation
    if len(shards) > 0:
        array = level_of(key, dims, shards, -0.22, 0.18) * array
    return jnp.clip(array, min=-bound, max=bound).astype(kind)


def heavy_noise(own_key, dims, deviation, reach, cuts, heavy, held_as=jnp.bfloat16):
    drawn = deviation * jax.random.normal(own_key, dims, jnp.float32)
    if cuts:
        drawn = drawn * level_of(own_key, dims, cuts, -0.22, 0.18)
    return jnp.clip(raised(drawn, jax.random.fold_in(own_key, 3), *heavy), -reach, reach).astype(held_as)


def setup_inputs(seed: int = 0, part: int = 0) -> dict:
    key_list = jax.random.split(jax.random.key(seed), 9)
    part_keys = jax.random.split(jax.random.fold_in(key_list[8], part), 9)
    inputs = centred(part_keys[0], (DOCS, LEN, D), 1.0, 6.0, ((0, 2), (1, 8)))
    out_grads = centred(part_keys[1], (DOCS, LEN, D), 1.0, 6.0, ((0, 2), (1, 8)))
    doc_lengths = draw_doc_lengths(jax.random.fold_in(jax.random.fold_in(key_list[8], part), 71), part)
    in_proj = centred(key_list[3], (D, R), D ** -0.5, 0.09375)
    out_proj = centred(key_list[4], (D, R), D ** -0.5, 0.09375)
    in_factor = draw_in_factor(jax.random.fold_in(key_list[8], 71), part)
    out_factor = draw_out_factor(jax.random.fold_in(key_list[8], 71), part)
    index_rows = heavy_noise(part_keys[7], (ROWS, F), (F * LEN) ** -0.5, 0.00048828125, ((1, 16),), (1, 0, 16, 2.0))
    return {"inputs": inputs, "out_grads": out_grads, "doc_lengths": doc_lengths, "in_proj": in_proj, "out_proj": out_proj, "in_factor": in_factor, "out_factor": out_factor, "index_rows": index_rows}


def reference(inputs, out_grads, doc_lengths, in_proj, out_proj, in_factor, out_factor, index_rows):
    positions = jnp.arange(LEN, dtype=jnp.int32)

    def per_document(operands):
        act_rows, grad_rows, length = operands
        in_rows = jnp.dot(act_rows, in_proj, preferred_element_type=jnp.float32).astype(jnp.bfloat16)
        out_rows = jnp.dot(grad_rows, out_proj, preferred_element_type=jnp.float32).astype(jnp.bfloat16)
        live = (positions < length).astype(jnp.bfloat16)
        masked = out_rows * live[:, None]
        grad = jnp.dot(masked.T, in_rows, preferred_element_type=jnp.float32)
        left = jnp.dot(out_factor, grad, precision=lax.Precision.HIGHEST)
        precond = jnp.dot(left, in_factor, precision=lax.Precision.HIGHEST)
        return precond.reshape(-1).astype(jnp.bfloat16)

    precond = lax.map(per_document, (inputs, out_grads, doc_lengths))
    return jnp.dot(index_rows, precond.T, preferred_element_type=jnp.float32)
```

```python
import jax
import jax.numpy as jnp
from jax import lax
from jax.sharding import PartitionSpec as P

HI = lax.Precision.HIGHEST


def on_device(inputs, out_grads, doc_lengths, in_proj, out_proj, in_factor, out_factor, index_rows):
    doc_count, tok_count, model_width = inputs.shape
    rank_size = in_proj.shape[1]
    part_size = lax.axis_size(("seq", "sub"))
    rep_size = lax.axis_size("rep")
    owner_count = part_size * rep_size
    offset = lax.axis_index(("seq", "sub")) * tok_count
    positions = offset + jnp.arange(tok_count, dtype=jnp.int32)
    live = positions[None, :] < doc_lengths[:, None]
    in_rows = jnp.dot(
        inputs.reshape(-1, model_width), in_proj, preferred_element_type=jnp.float32
    ).astype(jnp.bfloat16)
    out_rows = jnp.dot(
        out_grads.reshape(-1, model_width), out_proj, preferred_element_type=jnp.float32
    ).astype(jnp.bfloat16)
    in_rows = in_rows.reshape(doc_count, tok_count, rank_size)
    out_rows = out_rows.reshape(doc_count, tok_count, rank_size)
    out_rows = jnp.where(live[:, :, None], out_rows, jnp.zeros_like(out_rows))
    grad = jnp.einsum("dto,dti->doi", out_rows, in_rows, preferred_element_type=jnp.float32)
    left = jnp.einsum("po,doi->dpi", out_factor, grad, precision=HI)
    part = jnp.einsum("dpi,iq->dpq", left, in_factor, precision=HI).astype(jnp.bfloat16)
    part = part.reshape(doc_count, owner_count, rank_size // owner_count, rank_size)
    part = part.transpose(1, 0, 2, 3)
    got = lax.all_to_all(part, ("seq", "sub", "rep"), split_axis=0, concat_axis=0, tiled=True)
    got = got.reshape(part_size, rep_size * doc_count, -1)
    precond = jnp.sum(got.astype(jnp.float32), axis=0).astype(jnp.bfloat16)
    scores = lax.dot_general(
        precond, index_rows, (((1,), (1,)), ((), ())), preferred_element_type=jnp.float32
    )
    rows = scores.shape[1] // owner_count
    scores = scores.reshape(-1, owner_count, rows).transpose(1, 0, 2)
    mine = lax.all_to_all(scores, ("seq", "sub", "rep"), split_axis=0, concat_axis=0, tiled=True)
    return jnp.sum(mine, axis=0).T


def solution(mesh):
    in_specs = (
        P(("grp", "rep"), ("seq", "sub"), None),
        P(("grp", "rep"), ("seq", "sub"), None),
        P(("grp", "rep")),
        P(),
        P(),
        P(),
        P(),
        P("grp", ("seq", "sub", "rep")),
    )
    out_specs = P(("grp", "seq", "sub", "rep"), None)
    return jax.shard_map(
        on_device, mesh=mesh, in_specs=in_specs, out_specs=out_specs, check_vma=False
    )
```

```python
import functools

import jax
import jax.numpy as jnp
from jax import lax
from jax.experimental import pallas as pl
from jax.experimental.pallas import tpu as pltpu
from jax.sharding import PartitionSpec as P

HI = lax.Precision.HIGHEST
BF16 = jnp.bfloat16
F32 = jnp.float32
OWNERS = ("seq", "sub", "rep")
FLIGHT = 2
SLOTS = 3
SCORED = 4


def halves(a):
    high = a.astype(BF16)
    return high, (a - high.astype(F32)).astype(BF16)


def dot(a, b):
    return jnp.dot(a, b, preferred_element_type=F32)


def dot3(a, b):
    return dot(a[0], b[0]) + (dot(a[0], b[1]) + dot(a[1], b[0]))


def in_hbm(array):
    return pltpu.with_memory_space_constraint(array, pltpu.HBM)


def spans(bits):
    found = [0]
    for bit in bits:
        found = found + [bit ^ f for f in found]
    return found


def groups():
    rep = lax.axis_size("rep")
    plane = rep * lax.axis_size("sub")
    return spans((rep, plane)), spans((2 * plane, 1))


def partial_kernel(first, second, lengths_hbm, x_hbm, g_hbm, pin_hbm, pout_hbm, factor_hbm, *rest):
    outs, rest = rest[: len(first)], rest[len(first) :]
    proj, held, kept_in, kept_out, grads, whole, factor, split, lengths, sems, once = rest
    slots, tok_count, _ = held.shape
    doc_count = x_hbm.shape[0]
    owned = outs[0].shape[2]
    part = lax.axis_index("seq") * lax.axis_size("sub") + lax.axis_index("sub")
    me = part * lax.axis_size("rep") + lax.axis_index("rep")
    base = part * tok_count
    items = 2 * doc_count

    def load(item, side):
        slot = lax.rem(item, slots)
        return pltpu.make_async_copy((x_hbm, g_hbm)[side].at[item // 2], held.at[slot], sems.at[slot])

    project = [
        pltpu.make_async_copy((pin_hbm, pout_hbm)[s], proj.at[s], once.at[s]) for s in range(2)
    ]
    small = [
        pltpu.make_async_copy(factor_hbm, factor, once.at[2]),
        pltpu.make_async_copy(lengths_hbm, lengths, once.at[3]),
    ]
    project[0].start()
    load(0, 0).start()
    load(1, 1).start()
    project[1].start()
    for copy in small:
        copy.start()
    project[0].wait()

    def scatter(doc, values, row):
        whole[...] = values
        for i, a in enumerate(first):
            for j, b in enumerate(second):
                start = pl.multiple_of((me ^ (a ^ b)) * owned, owned)
                outs[i][j, doc] = whole[pl.ds(start, owned), :].astype(BF16)

    def gradient(doc):
        return lax.dot_general(
            kept_out[...],
            kept_in[lax.rem(doc, 2)],
            (((0,), (0,)), ((), ())),
            preferred_element_type=F32,
        )

    def finish(doc):
        scatter(doc, dot3((split[0], split[1]), halves(gradient(doc))), 0)

    def one(item, carry):
        doc = item // 2
        side = lax.rem(item, 2)

        @pl.when(item == 1)
        def _():
            project[1].wait()
            for copy in small:
                copy.wait()
            split[0], split[1] = halves(factor[...])

        load(item, 0).wait()

        @pl.when((item + FLIGHT < items) & (side == 0))
        def _():
            load(item + FLIGHT, 0).start()

        @pl.when((item + FLIGHT < items) & (side == 1))
        def _():
            load(item + FLIGHT, 1).start()

        @pl.when(side == 0)
        def _():
            rows = dot(held[lax.rem(item, slots)], proj[0])
            kept_in[lax.rem(doc, 2)] = rows.astype(BF16)
            grads[jnp.maximum(doc - 1, 0)] = gradient(jnp.maximum(doc - 1, 0))

        @pl.when(side == 1)
        def _():
            rows = dot(held[lax.rem(item, slots)], proj[1])
            position = base + lax.broadcasted_iota(jnp.int32, rows.shape, 0)
            kept_out[...] = jnp.where(position < lengths[doc], rows, 0.0).astype(BF16)

        return carry

    lax.fori_loop(0, items, one, 0)
    grads[doc_count - 1] = gradient(doc_count - 1)
    for doc in range(doc_count):
        scatter(doc, dot3((split[0], split[1]), halves(grads[doc])), doc)


def partials(inputs, out_grads, doc_lengths, in_proj, out_proj, out_factor, first, second):
    doc_count, tok_count, width = inputs.shape
    rank = in_proj.shape[1]
    owned = rank // (len(first) * len(second))
    hbm = pl.BlockSpec(memory_space=pltpu.HBM)
    vmem = pl.BlockSpec(memory_space=pltpu.VMEM)
    return pl.pallas_call(
        functools.partial(partial_kernel, first, second),
        out_shape=[jax.ShapeDtypeStruct((len(second), doc_count, owned, rank), BF16)] * len(first),
        in_specs=[hbm] * 6,
        out_specs=[vmem] * len(first),
        scratch_shapes=[
            pltpu.VMEM((2, width, rank), BF16),
            pltpu.VMEM((SLOTS, tok_count, width), BF16),
            pltpu.VMEM((2, tok_count, rank), BF16),
            pltpu.VMEM((tok_count, rank), BF16),
            pltpu.VMEM((doc_count, rank, rank), F32),
            pltpu.VMEM((rank, rank), F32),
            pltpu.VMEM((rank, rank), F32),
            pltpu.VMEM((2, rank, rank), BF16),
            pltpu.SMEM((doc_count,), jnp.int32),
            pltpu.SemaphoreType.DMA((SLOTS,)),
            pltpu.SemaphoreType.DMA((4,)),
        ],
        compiler_params=pltpu.CompilerParams(vmem_limit_bytes=28 << 20),
        cost_estimate=pl.CostEstimate(
            flops=4 * doc_count * tok_count * width * rank,
            bytes_accessed=4 * doc_count * tok_count * width,
            transcendentals=0,
        ),
        name="partials",
    )(*map(in_hbm, (doc_lengths, inputs, out_grads, in_proj, out_proj, out_factor)))


def fetch_kernel(index_hbm, token, held, sems):
    pieces = sems.shape[0]
    rows = held.shape[0] // pieces
    spans = [pl.ds(i * rows, rows) for i in range(pieces)]
    copies = [
        pltpu.make_async_copy(index_hbm.at[span, :], held.at[span, :], sems.at[i])
        for i, span in enumerate(spans)
    ]
    for copy in copies:
        copy.start()
    for copy in copies:
        copy.wait()


def fetch(index_rows, count, token):
    pieces = 4
    width = index_rows.shape[1]
    size = count * width * index_rows.dtype.itemsize
    return pl.pallas_call(
        fetch_kernel,
        out_shape=jax.ShapeDtypeStruct((count, width), index_rows.dtype),
        in_specs=[pl.BlockSpec(memory_space=pltpu.HBM), pl.BlockSpec(memory_space=pl.ANY)],
        out_specs=pl.BlockSpec(memory_space=pltpu.VMEM),
        scratch_shapes=[pltpu.SemaphoreType.DMA((pieces,))],
        compiler_params=pltpu.CompilerParams(vmem_limit_bytes=1 << 20),
        cost_estimate=pl.CostEstimate(flops=0, bytes_accessed=2 * size, transcendentals=0),
        name="fetch",
    )(in_hbm(index_rows), token)


def score_kernel(total, factor, early, index_hbm, out, precond, late, sems):
    owners, _, owner_rows = out.shape
    owned, docs, rank = total.shape
    pieces = sems.shape[0]
    early_count = early.shape[0]
    rows = late.shape[0] // pieces
    copies = [
        pltpu.make_async_copy(
            index_hbm.at[pl.ds(early_count + i * rows, rows), :],
            late.at[pl.ds(i * rows, rows), :],
            sems.at[i],
        )
        for i in range(pieces)
    ]
    for copy in copies:
        copy.start()
    values = total[...].reshape(owned * docs, rank)
    values = dot3(halves(values), halves(factor[...])).astype(BF16)
    for o in range(owned):
        precond[:, o * rank : (o + 1) * rank] = values[o * docs : (o + 1) * docs]

    def scored(index, first):
        block = SCORED * owner_rows

        def one(k, carry):
            span = pl.ds(pl.multiple_of(k * block, block), block)
            scores = lax.dot_general(
                precond[...], index[span, :], (((1,), (1,)), ((), ())), preferred_element_type=F32
            )
            for j in range(SCORED):
                out[first + k * SCORED + j] = scores[:, j * owner_rows : (j + 1) * owner_rows]
            return carry

        lax.fori_loop(0, index.shape[0] // block, one, 0)

    scored(early, 0)
    for copy in copies:
        copy.wait()
    scored(late, early_count // owner_rows)


def score(total, in_factor, early, index_rows, owner_count):
    owned, docs, rank = total.shape
    rows, features = index_rows.shape
    late = rows - early.shape[0]
    pieces = 4
    vmem = pl.BlockSpec(memory_space=pltpu.VMEM)
    return pl.pallas_call(
        score_kernel,
        out_shape=jax.ShapeDtypeStruct((owner_count, docs, rows // owner_count), F32),
        in_specs=[vmem] * 3 + [pl.BlockSpec(memory_space=pltpu.HBM)],
        out_specs=vmem,
        scratch_shapes=[
            pltpu.VMEM((docs, features), BF16),
            pltpu.VMEM((late, features), BF16),
            pltpu.SemaphoreType.DMA((pieces,)),
        ],
        compiler_params=pltpu.CompilerParams(vmem_limit_bytes=24 << 20),
        cost_estimate=pl.CostEstimate(
            flops=2 * docs * rows * features, bytes_accessed=0, transcendentals=0
        ),
        name="score",
    )(total, in_factor, early, in_hbm(index_rows))


def to_partner(value, owner_count, offset):
    return lax.ppermute(value, OWNERS, [(i, i ^ offset) for i in range(owner_count)])


def fast(inputs, out_grads, doc_lengths, in_proj, out_proj, in_factor, out_factor, index_rows):
    owner_count = lax.axis_size(OWNERS)
    first, second = groups()
    pieces = partials(
        inputs, out_grads, doc_lengths, in_proj, out_proj, out_factor, first, second
    )
    got = [pieces[0]] + [
        to_partner(pieces[i], owner_count, first[i]) for i in range(1, len(first))
    ]
    sums = sum(g.astype(F32) for g in got).astype(BF16)
    rel = lax.optimization_barrier([sums[j] for j in range(len(second))])
    got = {
        second[j]: to_partner(rel[j], owner_count, second[j]) for j in range(1, len(second))
    }
    got[0] = rel[0]
    early = fetch(index_rows, index_rows.shape[0] // 2, rel[0])
    own = sum(got[b].astype(F32) for b in second if b % 2 == 0)
    other = sum(got[b].astype(F32) for b in second if b % 2 == 1)
    low = lax.axis_index("rep") == 0
    total = jnp.where(low, jnp.concatenate([own, other]), jnp.concatenate([other, own]))
    total = total.transpose(1, 0, 2)
    scores = score(total, in_factor, early, index_rows, owner_count)
    mine = lax.all_to_all(scores, OWNERS, split_axis=0, concat_axis=0, tiled=True)
    return jnp.sum(mine, axis=0).T


def plain(inputs, out_grads, doc_lengths, in_proj, out_proj, in_factor, out_factor, index_rows):
    doc_count, tok_count, model_width = inputs.shape
    rank_size = in_proj.shape[1]
    part_size = lax.axis_size(("seq", "sub"))
    rep_size = lax.axis_size("rep")
    owner_count = part_size * rep_size
    offset = lax.axis_index(("seq", "sub")) * tok_count
    positions = offset + jnp.arange(tok_count, dtype=jnp.int32)
    live = positions[None, :] < doc_lengths[:, None]
    in_rows = dot(inputs.reshape(-1, model_width), in_proj).astype(BF16)
    out_rows = dot(out_grads.reshape(-1, model_width), out_proj).astype(BF16)
    in_rows = in_rows.reshape(doc_count, tok_count, rank_size)
    out_rows = out_rows.reshape(doc_count, tok_count, rank_size)
    out_rows = jnp.where(live[:, :, None], out_rows, jnp.zeros_like(out_rows))
    grad = jnp.einsum("dto,dti->doi", out_rows, in_rows, preferred_element_type=F32)
    left = jnp.einsum("po,doi->dpi", out_factor, grad, precision=HI)
    part = jnp.einsum("dpi,iq->dpq", left, in_factor, precision=HI).astype(BF16)
    part = part.reshape(doc_count, owner_count, rank_size // owner_count, rank_size)
    part = part.transpose(1, 0, 2, 3)
    got = lax.all_to_all(part, OWNERS, split_axis=0, concat_axis=0, tiled=True)
    got = got.reshape(part_size, rep_size * doc_count, -1)
    precond = jnp.sum(got.astype(F32), axis=0).astype(BF16)
    scores = lax.dot_general(
        precond, index_rows, (((1,), (1,)), ((), ())), preferred_element_type=F32
    )
    rows = scores.shape[1] // owner_count
    scores = scores.reshape(-1, owner_count, rows).transpose(1, 0, 2)
    mine = lax.all_to_all(scores, OWNERS, split_axis=0, concat_axis=0, tiled=True)
    return jnp.sum(mine, axis=0).T


def on_device(*args):
    owner_count = lax.axis_size(OWNERS)
    rank_size = args[3].shape[1]
    sizes = tuple(lax.axis_size(axis) for axis in OWNERS)
    docs = sizes[2] * args[0].shape[0]
    if sizes == (4, 2, 2) and docs == 8 and rank_size % (16 * owner_count) == 0:
        return fast(*args)
    return plain(*args)


def solution(mesh):
    in_specs = (
        P(("grp", "rep"), ("seq", "sub"), None),
        P(("grp", "rep"), ("seq", "sub"), None),
        P(("grp", "rep")),
        P(),
        P(),
        P(),
        P(),
        P("grp", ("seq", "sub", "rep")),
    )
    out_specs = P(("grp", "seq", "sub", "rep"), None)
    return jax.shard_map(
        on_device, mesh=mesh, in_specs=in_specs, out_specs=out_specs, check_vma=False
    )
```

```python
import functools

import jax
import jax.numpy as jnp
from jax import lax
from jax.experimental import pallas as pl
from jax.experimental.pallas import tpu as pltpu
from jax.sharding import PartitionSpec as P

HI = lax.Precision.HIGHEST
BF16 = jnp.bfloat16
F32 = jnp.float32
OWNERS = ("seq", "sub", "rep")
FLIGHT = 3
SLOTS = 4
SCORED = 4


def halves(a):
    high = a.astype(BF16)
    return high, (a - high.astype(F32)).astype(BF16)


def dot(a, b):
    return jnp.dot(a, b, preferred_element_type=F32)


def dot3(a, b):
    return dot(a[0], b[0]) + (dot(a[0], b[1]) + dot(a[1], b[0]))


def in_hbm(array):
    return pltpu.with_memory_space_constraint(array, pltpu.HBM)


def spans(bits):
    found = [0]
    for bit in bits:
        found = found + [bit ^ f for f in found]
    return found


def groups():
    rep = lax.axis_size("rep")
    plane = rep * lax.axis_size("sub")
    return spans((rep, plane)), spans((2 * plane, 1))


def partial_kernel(first, second, lengths_hbm, x_hbm, g_hbm, pin_hbm, pout_hbm, factor_hbm, *rest):
    outs, rest = rest[: len(first)], rest[len(first) :]
    proj, held, kept_in, kept_out, grads, whole, factor, split, lengths, sems, once = rest
    slots, tok_count, _ = held.shape
    doc_count = x_hbm.shape[0]
    owned = outs[0].shape[2]
    part = lax.axis_index("seq") * lax.axis_size("sub") + lax.axis_index("sub")
    me = part * lax.axis_size("rep") + lax.axis_index("rep")
    base = part * tok_count
    items = 2 * doc_count

    def load(item, side):
        slot = lax.rem(item, slots)
        return pltpu.make_async_copy((x_hbm, g_hbm)[side].at[item // 2], held.at[slot], sems.at[slot])

    project = [
        pltpu.make_async_copy((pin_hbm, pout_hbm)[s], proj.at[s], once.at[s]) for s in range(2)
    ]
    small = [
        pltpu.make_async_copy(factor_hbm, factor, once.at[2]),
        pltpu.make_async_copy(lengths_hbm, lengths, once.at[3]),
    ]
    project[0].start()
    load(0, 0).start()
    load(1, 1).start()
    project[1].start()
    load(2, 0).start()
    for copy in small:
        copy.start()
    project[0].wait()

    def scatter(doc, values, row):
        whole[...] = values
        for i, a in enumerate(first):
            for j, b in enumerate(second):
                start = pl.multiple_of((me ^ (a ^ b)) * owned, owned)
                outs[i][j, doc] = whole[pl.ds(start, owned), :].astype(BF16)

    def gradient(doc):
        return lax.dot_general(
            kept_out[...],
            kept_in[lax.rem(doc, 2)],
            (((0,), (0,)), ((), ())),
            preferred_element_type=F32,
        )

    def finish(doc):
        scatter(doc, dot3((split[0], split[1]), halves(gradient(doc))), 0)

    def one(item, carry):
        doc = item // 2
        side = lax.rem(item, 2)

        @pl.when(item == 1)
        def _():
            project[1].wait()
            for copy in small:
                copy.wait()
            split[0], split[1] = halves(factor[...])

        load(item, 0).wait()

        @pl.when((item + FLIGHT < items) & (side == 1))
        def _():
            load(item + FLIGHT, 0).start()

        @pl.when((item + FLIGHT < items) & (side == 0))
        def _():
            load(item + FLIGHT, 1).start()

        @pl.when(side == 0)
        def _():
            rows = dot(held[lax.rem(item, slots)], proj[0])
            kept_in[lax.rem(doc, 2)] = rows.astype(BF16)
            grads[jnp.maximum(doc - 1, 0)] = gradient(jnp.maximum(doc - 1, 0))

        @pl.when(side == 1)
        def _():
            rows = dot(held[lax.rem(item, slots)], proj[1])
            position = base + lax.broadcasted_iota(jnp.int32, rows.shape, 0)
            kept_out[...] = jnp.where(position < lengths[doc], rows, 0.0).astype(BF16)

        return carry

    lax.fori_loop(0, items, one, 0)
    grads[doc_count - 1] = gradient(doc_count - 1)
    for doc in range(doc_count):
        scatter(doc, dot3((split[0], split[1]), halves(grads[doc])), doc)


def partials(inputs, out_grads, doc_lengths, in_proj, out_proj, out_factor, first, second):
    doc_count, tok_count, width = inputs.shape
    rank = in_proj.shape[1]
    owned = rank // (len(first) * len(second))
    hbm = pl.BlockSpec(memory_space=pltpu.HBM)
    vmem = pl.BlockSpec(memory_space=pltpu.VMEM)
    return pl.pallas_call(
        functools.partial(partial_kernel, first, second),
        out_shape=[jax.ShapeDtypeStruct((len(second), doc_count, owned, rank), BF16)] * len(first),
        in_specs=[hbm] * 6,
        out_specs=[vmem] * len(first),
        scratch_shapes=[
            pltpu.VMEM((2, width, rank), BF16),
            pltpu.VMEM((SLOTS, tok_count, width), BF16),
            pltpu.VMEM((2, tok_count, rank), BF16),
            pltpu.VMEM((tok_count, rank), BF16),
            pltpu.VMEM((doc_count, rank, rank), F32),
            pltpu.VMEM((rank, rank), F32),
            pltpu.VMEM((rank, rank), F32),
            pltpu.VMEM((2, rank, rank), BF16),
            pltpu.SMEM((doc_count,), jnp.int32),
            pltpu.SemaphoreType.DMA((SLOTS,)),
            pltpu.SemaphoreType.DMA((4,)),
        ],
        compiler_params=pltpu.CompilerParams(vmem_limit_bytes=32 << 20),
        cost_estimate=pl.CostEstimate(
            flops=4 * doc_count * tok_count * width * rank,
            bytes_accessed=4 * doc_count * tok_count * width,
            transcendentals=0,
        ),
        name="partials",
    )(*map(in_hbm, (doc_lengths, inputs, out_grads, in_proj, out_proj, out_factor)))


def fetch_kernel(index_hbm, token, held, sems):
    pieces = sems.shape[0]
    rows = held.shape[0] // pieces
    spans = [pl.ds(i * rows, rows) for i in range(pieces)]
    copies = [
        pltpu.make_async_copy(index_hbm.at[span, :], held.at[span, :], sems.at[i])
        for i, span in enumerate(spans)
    ]
    for copy in copies:
        copy.start()
    for copy in copies:
        copy.wait()


def fetch(index_rows, count, token):
    pieces = 4
    width = index_rows.shape[1]
    size = count * width * index_rows.dtype.itemsize
    return pl.pallas_call(
        fetch_kernel,
        out_shape=jax.ShapeDtypeStruct((count, width), index_rows.dtype),
        in_specs=[pl.BlockSpec(memory_space=pltpu.HBM), pl.BlockSpec(memory_space=pl.ANY)],
        out_specs=pl.BlockSpec(memory_space=pltpu.VMEM),
        scratch_shapes=[pltpu.SemaphoreType.DMA((pieces,))],
        compiler_params=pltpu.CompilerParams(vmem_limit_bytes=1 << 20),
        cost_estimate=pl.CostEstimate(flops=0, bytes_accessed=2 * size, transcendentals=0),
        name="fetch",
    )(in_hbm(index_rows), token)


def score_kernel(total, factor, early, index_hbm, out, precond, late, sems):
    owners, _, owner_rows = out.shape
    owned, docs, rank = total.shape
    pieces = sems.shape[0]
    early_count = early.shape[0]
    rows = late.shape[0] // pieces
    copies = [
        pltpu.make_async_copy(
            index_hbm.at[pl.ds(early_count + i * rows, rows), :],
            late.at[pl.ds(i * rows, rows), :],
            sems.at[i],
        )
        for i in range(pieces)
    ]
    for copy in copies:
        copy.start()
    values = total[...].reshape(owned * docs, rank)
    values = dot3(halves(values), halves(factor[...])).astype(BF16)
    for o in range(owned):
        precond[:, o * rank : (o + 1) * rank] = values[o * docs : (o + 1) * docs]

    def scored(index, first):
        block = SCORED * owner_rows

        def one(k, carry):
            span = pl.ds(pl.multiple_of(k * block, block), block)
            scores = lax.dot_general(
                precond[...], index[span, :], (((1,), (1,)), ((), ())), preferred_element_type=F32
            )
            for j in range(SCORED):
                out[first + k * SCORED + j] = scores[:, j * owner_rows : (j + 1) * owner_rows]
            return carry

        lax.fori_loop(0, index.shape[0] // block, one, 0)

    scored(early, 0)
    for copy in copies:
        copy.wait()
    scored(late, early_count // owner_rows)


def score(total, in_factor, early, index_rows, owner_count):
    owned, docs, rank = total.shape
    rows, features = index_rows.shape
    late = rows - early.shape[0]
    pieces = 4
    vmem = pl.BlockSpec(memory_space=pltpu.VMEM)
    return pl.pallas_call(
        score_kernel,
        out_shape=jax.ShapeDtypeStruct((owner_count, docs, rows // owner_count), F32),
        in_specs=[vmem] * 3 + [pl.BlockSpec(memory_space=pltpu.HBM)],
        out_specs=vmem,
        scratch_shapes=[
            pltpu.VMEM((docs, features), BF16),
            pltpu.VMEM((late, features), BF16),
            pltpu.SemaphoreType.DMA((pieces,)),
        ],
        compiler_params=pltpu.CompilerParams(vmem_limit_bytes=24 << 20),
        cost_estimate=pl.CostEstimate(
            flops=2 * docs * rows * features, bytes_accessed=0, transcendentals=0
        ),
        name="score",
    )(total, in_factor, early, in_hbm(index_rows))


def to_partner(value, owner_count, offset):
    return lax.ppermute(value, OWNERS, [(i, i ^ offset) for i in range(owner_count)])


def fast(inputs, out_grads, doc_lengths, in_proj, out_proj, in_factor, out_factor, index_rows):
    owner_count = lax.axis_size(OWNERS)
    first, second = groups()
    pieces = partials(
        inputs, out_grads, doc_lengths, in_proj, out_proj, out_factor, first, second
    )
    got = [pieces[0]] + [
        to_partner(pieces[i], owner_count, first[i]) for i in range(1, len(first))
    ]
    sums = sum(g.astype(F32) for g in got).astype(BF16)
    rel = lax.optimization_barrier([sums[j] for j in range(len(second))])
    got = {
        second[j]: to_partner(rel[j], owner_count, second[j]) for j in range(1, len(second))
    }
    got[0] = rel[0]
    early = fetch(index_rows, index_rows.shape[0] // 2, rel[0])
    own = sum(got[b].astype(F32) for b in second if b % 2 == 0)
    other = sum(got[b].astype(F32) for b in second if b % 2 == 1)
    low = lax.axis_index("rep") == 0
    total = jnp.where(low, jnp.concatenate([own, other]), jnp.concatenate([other, own]))
    total = total.transpose(1, 0, 2)
    scores = score(total, in_factor, early, index_rows, owner_count)
    mine = lax.all_to_all(scores, OWNERS, split_axis=0, concat_axis=0, tiled=True)
    return jnp.sum(mine, axis=0).T


def plain(inputs, out_grads, doc_lengths, in_proj, out_proj, in_factor, out_factor, index_rows):
    doc_count, tok_count, model_width = inputs.shape
    rank_size = in_proj.shape[1]
    part_size = lax.axis_size(("seq", "sub"))
    rep_size = lax.axis_size("rep")
    owner_count = part_size * rep_size
    offset = lax.axis_index(("seq", "sub")) * tok_count
    positions = offset + jnp.arange(tok_count, dtype=jnp.int32)
    live = positions[None, :] < doc_lengths[:, None]
    in_rows = dot(inputs.reshape(-1, model_width), in_proj).astype(BF16)
    out_rows = dot(out_grads.reshape(-1, model_width), out_proj).astype(BF16)
    in_rows = in_rows.reshape(doc_count, tok_count, rank_size)
    out_rows = out_rows.reshape(doc_count, tok_count, rank_size)
    out_rows = jnp.where(live[:, :, None], out_rows, jnp.zeros_like(out_rows))
    grad = jnp.einsum("dto,dti->doi", out_rows, in_rows, preferred_element_type=F32)
    left = jnp.einsum("po,doi->dpi", out_factor, grad, precision=HI)
    part = jnp.einsum("dpi,iq->dpq", left, in_factor, precision=HI).astype(BF16)
    part = part.reshape(doc_count, owner_count, rank_size // owner_count, rank_size)
    part = part.transpose(1, 0, 2, 3)
    got = lax.all_to_all(part, OWNERS, split_axis=0, concat_axis=0, tiled=True)
    got = got.reshape(part_size, rep_size * doc_count, -1)
    precond = jnp.sum(got.astype(F32), axis=0).astype(BF16)
    scores = lax.dot_general(
        precond, index_rows, (((1,), (1,)), ((), ())), preferred_element_type=F32
    )
    rows = scores.shape[1] // owner_count
    scores = scores.reshape(-1, owner_count, rows).transpose(1, 0, 2)
    mine = lax.all_to_all(scores, OWNERS, split_axis=0, concat_axis=0, tiled=True)
    return jnp.sum(mine, axis=0).T


def on_device(*args):
    owner_count = lax.axis_size(OWNERS)
    rank_size = args[3].shape[1]
    sizes = tuple(lax.axis_size(axis) for axis in OWNERS)
    docs = sizes[2] * args[0].shape[0]
    if sizes == (4, 2, 2) and docs == 8 and rank_size % (16 * owner_count) == 0:
        return fast(*args)
    return plain(*args)


def solution(mesh):
    in_specs = (
        P(("grp", "rep"), ("seq", "sub"), None),
        P(("grp", "rep"), ("seq", "sub"), None),
        P(("grp", "rep")),
        P(),
        P(),
        P(),
        P(),
        P("grp", ("seq", "sub", "rep")),
    )
    out_specs = P(("grp", "seq", "sub", "rep"), None)
    return jax.shard_map(
        on_device, mesh=mesh, in_specs=in_specs, out_specs=out_specs, check_vma=False
    )
```

```python
import functools

import jax
import jax.numpy as jnp
from jax import lax
from jax.experimental import pallas as pl
from jax.experimental.pallas import tpu as pltpu
from jax.sharding import PartitionSpec as P

HI = lax.Precision.HIGHEST
BF16 = jnp.bfloat16
F32 = jnp.float32
OWNERS = ("seq", "sub", "rep")
FLIGHT = 3
SLOTS = 4
SCORED = 4


def halves(a):
    high = a.astype(BF16)
    return high, (a - high.astype(F32)).astype(BF16)


def dot(a, b):
    return jnp.dot(a, b, preferred_element_type=F32)


def dot3(a, b):
    return dot(a[0], b[0]) + (dot(a[0], b[1]) + dot(a[1], b[0]))


def in_hbm(array):
    return pltpu.with_memory_space_constraint(array, pltpu.HBM)


def spans(bits):
    found = [0]
    for bit in bits:
        found = found + [bit ^ f for f in found]
    return found


def groups():
    rep = lax.axis_size("rep")
    plane = rep * lax.axis_size("sub")
    return spans((rep, plane)), spans((2 * plane, 1))


def partial_kernel(first, second, lengths_hbm, x_hbm, g_hbm, pin_hbm, pout_hbm, factor_hbm, *rest):
    outs, rest = rest[: len(first)], rest[len(first) :]
    proj, held, kept_in, kept_out, grads, whole, factor, split, lengths, sems, once = rest
    slots, tok_count, _ = held.shape
    doc_count = x_hbm.shape[0]
    owned = outs[0].shape[2]
    part = lax.axis_index("seq") * lax.axis_size("sub") + lax.axis_index("sub")
    me = part * lax.axis_size("rep") + lax.axis_index("rep")
    base = part * tok_count
    items = 2 * doc_count

    def load(item, side):
        slot = lax.rem(item, slots)
        return pltpu.make_async_copy((x_hbm, g_hbm)[side].at[item // 2], held.at[slot], sems.at[slot])

    project = [
        pltpu.make_async_copy((pin_hbm, pout_hbm)[s], proj.at[s], once.at[s]) for s in range(2)
    ]
    small = [
        pltpu.make_async_copy(factor_hbm, factor, once.at[2]),
        pltpu.make_async_copy(lengths_hbm, lengths, once.at[3]),
    ]
    project[0].start()
    load(0, 0).start()
    load(1, 1).start()
    project[1].start()
    load(2, 0).start()
    for copy in small:
        copy.start()
    project[0].wait()

    def scatter(doc, values, row):
        whole[...] = values
        for i, a in enumerate(first):
            for j, b in enumerate(second):
                start = pl.multiple_of((me ^ (a ^ b)) * owned, owned)
                outs[i][j, doc] = whole[pl.ds(start, owned), :].astype(BF16)

    def gradient(doc):
        return lax.dot_general(
            kept_out[...],
            kept_in[lax.rem(doc, 2)],
            (((0,), (0,)), ((), ())),
            preferred_element_type=F32,
        )

    def finish(doc):
        scatter(doc, dot3((split[0], split[1]), halves(gradient(doc))), 0)

    def one(item, carry):
        doc = item // 2
        side = lax.rem(item, 2)

        @pl.when(item == 1)
        def _():
            project[1].wait()
            for copy in small:
                copy.wait()
            split[0], split[1] = halves(factor[...])

        load(item, 0).wait()

        @pl.when((item + FLIGHT < items) & (side == 1))
        def _():
            load(item + FLIGHT, 0).start()

        @pl.when((item + FLIGHT < items) & (side == 0))
        def _():
            load(item + FLIGHT, 1).start()

        @pl.when(side == 0)
        def _():
            rows = dot(held[lax.rem(item, slots)], proj[0])
            kept_in[lax.rem(doc, 2)] = rows.astype(BF16)
            grads[jnp.maximum(doc - 1, 0)] = gradient(jnp.maximum(doc - 1, 0))

        @pl.when(side == 1)
        def _():
            rows = dot(held[lax.rem(item, slots)], proj[1])
            position = base + lax.broadcasted_iota(jnp.int32, rows.shape, 0)
            kept_out[...] = jnp.where(position < lengths[doc], rows, 0.0).astype(BF16)

        return carry

    lax.fori_loop(0, items, one, 0)
    grads[doc_count - 1] = gradient(doc_count - 1)
    for doc in range(doc_count):
        scatter(doc, dot3((split[0], split[1]), halves(grads[doc])), doc)


def partials(inputs, out_grads, doc_lengths, in_proj, out_proj, out_factor, first, second):
    doc_count, tok_count, width = inputs.shape
    rank = in_proj.shape[1]
    owned = rank // (len(first) * len(second))
    hbm = pl.BlockSpec(memory_space=pltpu.HBM)
    vmem = pl.BlockSpec(memory_space=pltpu.VMEM)
    return pl.pallas_call(
        functools.partial(partial_kernel, first, second),
        out_shape=[jax.ShapeDtypeStruct((len(second), doc_count, owned, rank), BF16)] * len(first),
        in_specs=[hbm] * 6,
        out_specs=[vmem] * len(first),
        scratch_shapes=[
            pltpu.VMEM((2, width, rank), BF16),
            pltpu.VMEM((SLOTS, tok_count, width), BF16),
            pltpu.VMEM((2, tok_count, rank), BF16),
            pltpu.VMEM((tok_count, rank), BF16),
            pltpu.VMEM((doc_count, rank, rank), F32),
            pltpu.VMEM((rank, rank), F32),
            pltpu.VMEM((rank, rank), F32),
            pltpu.VMEM((2, rank, rank), BF16),
            pltpu.SMEM((doc_count,), jnp.int32),
            pltpu.SemaphoreType.DMA((SLOTS,)),
            pltpu.SemaphoreType.DMA((4,)),
        ],
        compiler_params=pltpu.CompilerParams(vmem_limit_bytes=32 << 20),
        cost_estimate=pl.CostEstimate(
            flops=4 * doc_count * tok_count * width * rank,
            bytes_accessed=4 * doc_count * tok_count * width,
            transcendentals=0,
        ),
        name="partials",
    )(*map(in_hbm, (doc_lengths, inputs, out_grads, in_proj, out_proj, out_factor)))


def score_kernel(block, total, factor, index, out, precond):
    owner_rows = out.shape[2]
    owned, docs, rank = total.shape
    values = total[...]
    swapped = jnp.concatenate([values[:, docs // 2 :], values[:, : docs // 2]], axis=1)
    values = jnp.where(lax.axis_index("rep") == 0, values, swapped)
    rows = values.reshape(owned * docs, rank)
    rows = dot3(halves(rows), halves(factor[...])).astype(BF16)
    for o in range(owned):
        precond[:, o * rank : (o + 1) * rank] = rows[o * docs : (o + 1) * docs]

    def one(k, carry):
        span = pl.ds(pl.multiple_of(k * block * owner_rows, block * owner_rows), block * owner_rows)
        scores = lax.dot_general(
            precond[...], index[span, :], (((1,), (1,)), ((), ())), preferred_element_type=F32
        )
        for j in range(block):
            out[k * block + j] = scores[:, j * owner_rows : (j + 1) * owner_rows]
        return carry

    lax.fori_loop(0, out.shape[0] // block, one, 0)


def score(total, in_factor, index_rows, owner_count):
    owned, docs, rank = total.shape
    rows, features = index_rows.shape
    vmem = pl.BlockSpec(memory_space=pltpu.VMEM)
    return pl.pallas_call(
        functools.partial(score_kernel, 4),
        out_shape=jax.ShapeDtypeStruct((owner_count, docs, rows // owner_count), F32),
        in_specs=[vmem] * 3,
        out_specs=vmem,
        scratch_shapes=[pltpu.VMEM((docs, features), BF16)],
        compiler_params=pltpu.CompilerParams(vmem_limit_bytes=8 << 20),
        cost_estimate=pl.CostEstimate(
            flops=2 * docs * rows * features, bytes_accessed=0, transcendentals=0
        ),
        name="score",
    )(total, in_factor, index_rows)


def to_partner(value, owner_count, offset):
    return lax.ppermute(value, OWNERS, [(i, i ^ offset) for i in range(owner_count)])


def fast(inputs, out_grads, doc_lengths, in_proj, out_proj, in_factor, out_factor, index_rows):
    owner_count = lax.axis_size(OWNERS)
    first, second = groups()
    pieces = partials(
        inputs, out_grads, doc_lengths, in_proj, out_proj, out_factor, first, second
    )
    got = [pieces[0]] + [
        to_partner(pieces[i], owner_count, first[i]) for i in range(1, len(first))
    ]
    sums = sum(g.astype(F32) for g in got).astype(BF16)
    rel = lax.optimization_barrier([sums[j] for j in range(len(second))])
    got = {
        second[j]: to_partner(rel[j], owner_count, second[j]) for j in range(1, len(second))
    }
    got[0] = rel[0]
    own = sum(got[b].astype(F32) for b in second if b % 2 == 0)
    other = sum(got[b].astype(F32) for b in second if b % 2 == 1)
    total = jnp.concatenate([own, other]).transpose(1, 0, 2)
    scores = score(total, in_factor, index_rows, owner_count)
    mine = lax.all_to_all(scores, OWNERS, split_axis=0, concat_axis=0, tiled=True)
    return jnp.sum(mine, axis=0).T


def plain(inputs, out_grads, doc_lengths, in_proj, out_proj, in_factor, out_factor, index_rows):
    doc_count, tok_count, model_width = inputs.shape
    rank_size = in_proj.shape[1]
    part_size = lax.axis_size(("seq", "sub"))
    rep_size = lax.axis_size("rep")
    owner_count = part_size * rep_size
    offset = lax.axis_index(("seq", "sub")) * tok_count
    positions = offset + jnp.arange(tok_count, dtype=jnp.int32)
    live = positions[None, :] < doc_lengths[:, None]
    in_rows = dot(inputs.reshape(-1, model_width), in_proj).astype(BF16)
    out_rows = dot(out_grads.reshape(-1, model_width), out_proj).astype(BF16)
    in_rows = in_rows.reshape(doc_count, tok_count, rank_size)
    out_rows = out_rows.reshape(doc_count, tok_count, rank_size)
    out_rows = jnp.where(live[:, :, None], out_rows, jnp.zeros_like(out_rows))
    grad = jnp.einsum("dto,dti->doi", out_rows, in_rows, preferred_element_type=F32)
    left = jnp.einsum("po,doi->dpi", out_factor, grad, precision=HI)
    part = jnp.einsum("dpi,iq->dpq", left, in_factor, precision=HI).astype(BF16)
    part = part.reshape(doc_count, owner_count, rank_size // owner_count, rank_size)
    part = part.transpose(1, 0, 2, 3)
    got = lax.all_to_all(part, OWNERS, split_axis=0, concat_axis=0, tiled=True)
    got = got.reshape(part_size, rep_size * doc_count, -1)
    precond = jnp.sum(got.astype(F32), axis=0).astype(BF16)
    scores = lax.dot_general(
        precond, index_rows, (((1,), (1,)), ((), ())), preferred_element_type=F32
    )
    rows = scores.shape[1] // owner_count
    scores = scores.reshape(-1, owner_count, rows).transpose(1, 0, 2)
    mine = lax.all_to_all(scores, OWNERS, split_axis=0, concat_axis=0, tiled=True)
    return jnp.sum(mine, axis=0).T


def on_device(*args):
    owner_count = lax.axis_size(OWNERS)
    rank_size = args[3].shape[1]
    sizes = tuple(lax.axis_size(axis) for axis in OWNERS)
    docs = sizes[2] * args[0].shape[0]
    if sizes == (4, 2, 2) and docs == 8 and rank_size % (16 * owner_count) == 0:
        return fast(*args)
    return plain(*args)


def solution(mesh):
    in_specs = (
        P(("grp", "rep"), ("seq", "sub"), None),
        P(("grp", "rep"), ("seq", "sub"), None),
        P(("grp", "rep")),
        P(),
        P(),
        P(),
        P(),
        P("grp", ("seq", "sub", "rep")),
    )
    out_specs = P(("grp", "seq", "sub", "rep"), None)
    return jax.shard_map(
        on_device, mesh=mesh, in_specs=in_specs, out_specs=out_specs, check_vma=False
    )
```

```python
import functools

import jax
import jax.numpy as jnp
from jax import lax
from jax.experimental import pallas as pl
from jax.experimental.pallas import tpu as pltpu
from jax.sharding import PartitionSpec as P

HI = lax.Precision.HIGHEST
BF16 = jnp.bfloat16
F32 = jnp.float32
OWNERS = ("seq", "sub", "rep")
FLIGHT = 3
SLOTS = 4
SCORED = 4
LANES = 128


def halves(a):
    high = a.astype(BF16)
    return high, (a - high.astype(F32)).astype(BF16)


def dot(a, b):
    return jnp.dot(a, b, preferred_element_type=F32)


def dot3(a, b):
    return dot(a[0], b[0]) + (dot(a[0], b[1]) + dot(a[1], b[0]))


def in_hbm(array):
    return pltpu.with_memory_space_constraint(array, pltpu.HBM)


def spans(bits):
    found = [0]
    for bit in bits:
        found = found + [bit ^ f for f in found]
    return found


def groups():
    rep = lax.axis_size("rep")
    plane = rep * lax.axis_size("sub")
    return spans((rep, plane)), spans((2 * plane, 1))


def partial_kernel(first, second, lengths_hbm, x_hbm, g_hbm, pin_hbm, pout_hbm, factor_hbm, *rest):
    outs, rest = rest[: len(first)], rest[len(first) :]
    proj, held, kept_in, kept_out, grads, whole, factor, split, lengths, sems, once = rest
    slots, tok_count, _ = held.shape
    doc_count = x_hbm.shape[0]
    owned = outs[0].shape[2]
    part = lax.axis_index("seq") * lax.axis_size("sub") + lax.axis_index("sub")
    me = part * lax.axis_size("rep") + lax.axis_index("rep")
    base = part * tok_count
    items = 2 * doc_count

    def load(item, side):
        slot = lax.rem(item, slots)
        return pltpu.make_async_copy((x_hbm, g_hbm)[side].at[item // 2], held.at[slot], sems.at[slot])

    project = [
        pltpu.make_async_copy((pin_hbm, pout_hbm)[s], proj.at[s], once.at[s]) for s in range(2)
    ]
    small = [
        pltpu.make_async_copy(factor_hbm, factor, once.at[2]),
        pltpu.make_async_copy(lengths_hbm, lengths, once.at[3]),
    ]
    project[0].start()
    load(0, 0).start()
    load(1, 1).start()
    project[1].start()
    load(2, 0).start()
    for copy in small:
        copy.start()
    project[0].wait()

    def scatter(doc, values, row):
        whole[...] = values
        for i, a in enumerate(first):
            for j, b in enumerate(second):
                start = pl.multiple_of((me ^ (a ^ b)) * owned, owned)
                outs[i][j, doc] = whole[pl.ds(start, owned), :].astype(BF16)

    def gradient(doc):
        return lax.dot_general(
            kept_out[...],
            kept_in[lax.rem(doc, 2)],
            (((0,), (0,)), ((), ())),
            preferred_element_type=F32,
        )

    def finish(doc):
        scatter(doc, dot3((split[0], split[1]), halves(gradient(doc))), 0)

    def one(item, carry):
        doc = item // 2
        side = lax.rem(item, 2)

        @pl.when(item == 1)
        def _():
            project[1].wait()
            for copy in small:
                copy.wait()
            split[0], split[1] = halves(factor[...])

        load(item, 0).wait()

        @pl.when((item + FLIGHT < items) & (side == 1))
        def _():
            load(item + FLIGHT, 0).start()

        @pl.when((item + FLIGHT < items) & (side == 0))
        def _():
            load(item + FLIGHT, 1).start()

        @pl.when(side == 0)
        def _():
            rows = dot(held[lax.rem(item, slots)], proj[0])
            kept_in[lax.rem(doc, 2)] = rows.astype(BF16)
            grads[jnp.maximum(doc - 1, 0)] = gradient(jnp.maximum(doc - 1, 0))

        @pl.when(side == 1)
        def _():
            rows = dot(held[lax.rem(item, slots)], proj[1])
            position = base + lax.broadcasted_iota(jnp.int32, rows.shape, 0)
            kept_out[...] = jnp.where(position < lengths[doc], rows, 0.0).astype(BF16)

        return carry

    lax.fori_loop(0, items, one, 0)
    grads[doc_count - 1] = gradient(doc_count - 1)
    for doc in range(doc_count):
        scatter(doc, dot3((split[0], split[1]), halves(grads[doc])), doc)


def partials(inputs, out_grads, doc_lengths, in_proj, out_proj, out_factor, first, second):
    doc_count, tok_count, width = inputs.shape
    rank = in_proj.shape[1]
    owned = rank // (len(first) * len(second))
    hbm = pl.BlockSpec(memory_space=pltpu.HBM)
    vmem = pl.BlockSpec(memory_space=pltpu.VMEM)
    return pl.pallas_call(
        functools.partial(partial_kernel, first, second),
        out_shape=[jax.ShapeDtypeStruct((len(second), doc_count, owned, rank), BF16)] * len(first),
        in_specs=[hbm] * 6,
        out_specs=[vmem] * len(first),
        scratch_shapes=[
            pltpu.VMEM((2, width, rank), BF16),
            pltpu.VMEM((SLOTS, tok_count, width), BF16),
            pltpu.VMEM((2, tok_count, rank), BF16),
            pltpu.VMEM((tok_count, rank), BF16),
            pltpu.VMEM((doc_count, rank, rank), F32),
            pltpu.VMEM((rank, rank), F32),
            pltpu.VMEM((rank, rank), F32),
            pltpu.VMEM((2, rank, rank), BF16),
            pltpu.SMEM((doc_count,), jnp.int32),
            pltpu.SemaphoreType.DMA((SLOTS,)),
            pltpu.SemaphoreType.DMA((4,)),
        ],
        compiler_params=pltpu.CompilerParams(vmem_limit_bytes=32 << 20),
        cost_estimate=pl.CostEstimate(
            flops=4 * doc_count * tok_count * width * rank,
            bytes_accessed=4 * doc_count * tok_count * width,
            transcendentals=0,
        ),
        name="partials",
    )(*map(in_hbm, (doc_lengths, inputs, out_grads, in_proj, out_proj, out_factor)))


def score_kernel(own, other, factor, index, out, applied, precond):
    owners, docs, owner_rows = out.shape
    part_docs, owned, rank = own[0].shape
    block = SCORED * owner_rows
    rows = part_docs * owned
    rep = lax.axis_index("rep")
    split = halves(factor[...])
    for pieces, place in ((own, rep), (other, 1 - rep)):
        total = sum(piece[...].astype(F32) for piece in pieces).reshape(rows, rank)
        total = dot3(halves(total), split)
        for lane in range(applied.shape[0]):
            applied[lane, pl.ds(pl.multiple_of(place * rows, rows), rows), :] = total[
                :, lane * LANES : (lane + 1) * LANES
            ]
    for o in range(owned):
        for lane in range(applied.shape[0]):
            start = o * rank + lane * LANES
            column = applied[lane, pl.ds(o, docs, stride=owned), :]
            precond[:, start : start + LANES] = column.astype(BF16)

    def one(k, carry):
        span = pl.ds(pl.multiple_of(k * block, block), block)
        scores = lax.dot_general(
            precond[...], index[span, :], (((1,), (1,)), ((), ())), preferred_element_type=F32
        )
        for j in range(SCORED):
            out[k * SCORED + j] = scores[:, j * owner_rows : (j + 1) * owner_rows]
        return carry

    lax.fori_loop(0, owners // SCORED, one, 0)


def score(own, other, in_factor, index_rows, owner_count):
    part_docs, owned, rank = own[0].shape
    docs = 2 * part_docs
    rows, features = index_rows.shape
    count = len(own)

    def kernel(*refs):
        score_kernel(refs[:count], refs[count : 2 * count], *refs[2 * count :])

    vmem = pl.BlockSpec(memory_space=pltpu.VMEM)
    return pl.pallas_call(
        kernel,
        out_shape=jax.ShapeDtypeStruct((owner_count, docs, rows // owner_count), F32),
        in_specs=[vmem] * (2 * count + 2),
        out_specs=vmem,
        scratch_shapes=[pltpu.VMEM((rank // LANES, docs * owned, LANES), F32), pltpu.VMEM((docs, features), BF16)],
        compiler_params=pltpu.CompilerParams(vmem_limit_bytes=8 << 20),
        cost_estimate=pl.CostEstimate(
            flops=2 * docs * rows * features, bytes_accessed=0, transcendentals=0
        ),
        name="score",
    )(*own, *other, in_factor, index_rows)


def to_partner(value, owner_count, offset):
    return lax.ppermute(value, OWNERS, [(i, i ^ offset) for i in range(owner_count)])


def fast(inputs, out_grads, doc_lengths, in_proj, out_proj, in_factor, out_factor, index_rows):
    owner_count = lax.axis_size(OWNERS)
    first, second = groups()
    pieces = partials(
        inputs, out_grads, doc_lengths, in_proj, out_proj, out_factor, first, second
    )
    got = [to_partner(pieces[i], owner_count, first[i]) for i in (2, 1, 3)] + [pieces[0]]
    sums = sum(g.astype(F32) for g in got).astype(BF16)
    rel = lax.optimization_barrier([sums[j] for j in range(len(second))])
    got = {
        second[j]: to_partner(rel[j], owner_count, second[j]) for j in range(1, len(second))
    }
    got[0] = rel[0]
    own = [got[b] for b in second if b % 2 == 0]
    other = [got[b] for b in second if b % 2 == 1]
    scores = score(own, other, in_factor, index_rows, owner_count)
    mine = lax.all_to_all(scores, OWNERS, split_axis=0, concat_axis=0, tiled=True)
    return jnp.sum(mine, axis=0).T


def plain(inputs, out_grads, doc_lengths, in_proj, out_proj, in_factor, out_factor, index_rows):
    doc_count, tok_count, model_width = inputs.shape
    rank_size = in_proj.shape[1]
    part_size = lax.axis_size(("seq", "sub"))
    rep_size = lax.axis_size("rep")
    owner_count = part_size * rep_size
    offset = lax.axis_index(("seq", "sub")) * tok_count
    positions = offset + jnp.arange(tok_count, dtype=jnp.int32)
    live = positions[None, :] < doc_lengths[:, None]
    in_rows = dot(inputs.reshape(-1, model_width), in_proj).astype(BF16)
    out_rows = dot(out_grads.reshape(-1, model_width), out_proj).astype(BF16)
    in_rows = in_rows.reshape(doc_count, tok_count, rank_size)
    out_rows = out_rows.reshape(doc_count, tok_count, rank_size)
    out_rows = jnp.where(live[:, :, None], out_rows, jnp.zeros_like(out_rows))
    grad = jnp.einsum("dto,dti->doi", out_rows, in_rows, preferred_element_type=F32)
    left = jnp.einsum("po,doi->dpi", out_factor, grad, precision=HI)
    part = jnp.einsum("dpi,iq->dpq", left, in_factor, precision=HI).astype(BF16)
    part = part.reshape(doc_count, owner_count, rank_size // owner_count, rank_size)
    part = part.transpose(1, 0, 2, 3)
    got = lax.all_to_all(part, OWNERS, split_axis=0, concat_axis=0, tiled=True)
    got = got.reshape(part_size, rep_size * doc_count, -1)
    precond = jnp.sum(got.astype(F32), axis=0).astype(BF16)
    scores = lax.dot_general(
        precond, index_rows, (((1,), (1,)), ((), ())), preferred_element_type=F32
    )
    rows = scores.shape[1] // owner_count
    scores = scores.reshape(-1, owner_count, rows).transpose(1, 0, 2)
    mine = lax.all_to_all(scores, OWNERS, split_axis=0, concat_axis=0, tiled=True)
    return jnp.sum(mine, axis=0).T


def on_device(*args):
    owner_count = lax.axis_size(OWNERS)
    rank_size = args[3].shape[1]
    sizes = tuple(lax.axis_size(axis) for axis in OWNERS)
    docs = sizes[2] * args[0].shape[0]
    if sizes == (4, 2, 2) and docs == 8 and rank_size % (16 * owner_count) == 0:
        return fast(*args)
    return plain(*args)


def solution(mesh):
    in_specs = (
        P(("grp", "rep"), ("seq", "sub"), None),
        P(("grp", "rep"), ("seq", "sub"), None),
        P(("grp", "rep")),
        P(),
        P(),
        P(),
        P(),
        P("grp", ("seq", "sub", "rep")),
    )
    out_specs = P(("grp", "seq", "sub", "rep"), None)
    return jax.shard_map(
        on_device, mesh=mesh, in_specs=in_specs, out_specs=out_specs, check_vma=False
    )
```

```python
import functools

import jax
import jax.numpy as jnp
from jax import lax
from jax.experimental import pallas as pl
from jax.experimental.pallas import tpu as pltpu
from jax.sharding import PartitionSpec as P

HI = lax.Precision.HIGHEST
BF16 = jnp.bfloat16
F32 = jnp.float32
OWNERS = ("seq", "sub", "rep")
FLIGHT = 3
SLOTS = 4
SCORED = 16
LANES = 128


def halves(a):
    high = a.astype(BF16)
    return high, (a - high.astype(F32)).astype(BF16)


def dot(a, b):
    return jnp.dot(a, b, preferred_element_type=F32)


def dot3(a, b):
    return dot(a[0], b[0]) + (dot(a[0], b[1]) + dot(a[1], b[0]))


def in_hbm(array):
    return pltpu.with_memory_space_constraint(array, pltpu.HBM)


def spans(bits):
    found = [0]
    for bit in bits:
        found = found + [bit ^ f for f in found]
    return found


def groups():
    rep = lax.axis_size("rep")
    plane = rep * lax.axis_size("sub")
    return spans((rep, plane)), spans((2 * plane, 1))


def partial_kernel(first, second, lengths_hbm, x_hbm, g_hbm, pin_hbm, pout_hbm, factor_hbm, *rest):
    outs, rest = rest[: len(first)], rest[len(first) :]
    proj, held, kept_in, kept_out, grads, whole, factor, split, lengths, sems, once = rest
    slots, tok_count, _ = held.shape
    doc_count = x_hbm.shape[0]
    owned = outs[0].shape[2]
    part = lax.axis_index("seq") * lax.axis_size("sub") + lax.axis_index("sub")
    me = part * lax.axis_size("rep") + lax.axis_index("rep")
    base = part * tok_count
    items = 2 * doc_count

    def load(item, side):
        slot = lax.rem(item, slots)
        return pltpu.make_async_copy((x_hbm, g_hbm)[side].at[item // 2], held.at[slot], sems.at[slot])

    project = [
        pltpu.make_async_copy((pin_hbm, pout_hbm)[s], proj.at[s], once.at[s]) for s in range(2)
    ]
    small = [
        pltpu.make_async_copy(factor_hbm, factor, once.at[2]),
        pltpu.make_async_copy(lengths_hbm, lengths, once.at[3]),
    ]
    project[0].start()
    load(0, 0).start()
    load(1, 1).start()
    project[1].start()
    load(2, 0).start()
    for copy in small:
        copy.start()
    project[0].wait()

    def scatter(doc, values, row):
        whole[...] = values
        for i, a in enumerate(first):
            for j, b in enumerate(second):
                start = pl.multiple_of((me ^ (a ^ b)) * owned, owned)
                outs[i][j, doc] = whole[pl.ds(start, owned), :].astype(BF16)

    def gradient(doc):
        return lax.dot_general(
            kept_out[...],
            kept_in[lax.rem(doc, 2)],
            (((0,), (0,)), ((), ())),
            preferred_element_type=F32,
        )

    def finish(doc):
        scatter(doc, dot3((split[0], split[1]), halves(gradient(doc))), 0)

    def one(item, carry):
        doc = item // 2
        side = lax.rem(item, 2)

        @pl.when(item == 1)
        def _():
            project[1].wait()
            for copy in small:
                copy.wait()
            split[0], split[1] = halves(factor[...])

        load(item, 0).wait()

        @pl.when((item + FLIGHT < items) & (side == 1))
        def _():
            load(item + FLIGHT, 0).start()

        @pl.when((item + FLIGHT < items) & (side == 0))
        def _():
            load(item + FLIGHT, 1).start()

        @pl.when(side == 0)
        def _():
            rows = dot(held[lax.rem(item, slots)], proj[0])
            kept_in[lax.rem(doc, 2)] = rows.astype(BF16)
            grads[jnp.maximum(doc - 1, 0)] = gradient(jnp.maximum(doc - 1, 0))

        @pl.when(side == 1)
        def _():
            rows = dot(held[lax.rem(item, slots)], proj[1])
            position = base + lax.broadcasted_iota(jnp.int32, rows.shape, 0)
            kept_out[...] = jnp.where(position < lengths[doc], rows, 0.0).astype(BF16)

        return carry

    lax.fori_loop(0, items, one, 0)
    grads[doc_count - 1] = gradient(doc_count - 1)
    for doc in range(doc_count):
        scatter(doc, dot3((split[0], split[1]), halves(grads[doc])), doc)


def partials(inputs, out_grads, doc_lengths, in_proj, out_proj, out_factor, first, second):
    doc_count, tok_count, width = inputs.shape
    rank = in_proj.shape[1]
    owned = rank // (len(first) * len(second))
    hbm = pl.BlockSpec(memory_space=pltpu.HBM)
    vmem = pl.BlockSpec(memory_space=pltpu.VMEM)
    return pl.pallas_call(
        functools.partial(partial_kernel, first, second),
        out_shape=[jax.ShapeDtypeStruct((len(second), doc_count, owned, rank), BF16)] * len(first),
        in_specs=[hbm] * 6,
        out_specs=[vmem] * len(first),
        scratch_shapes=[
            pltpu.VMEM((2, width, rank), BF16),
            pltpu.VMEM((SLOTS, tok_count, width), BF16),
            pltpu.VMEM((2, tok_count, rank), BF16),
            pltpu.VMEM((tok_count, rank), BF16),
            pltpu.VMEM((doc_count, rank, rank), F32),
            pltpu.VMEM((rank, rank), F32),
            pltpu.VMEM((rank, rank), F32),
            pltpu.VMEM((2, rank, rank), BF16),
            pltpu.SMEM((doc_count,), jnp.int32),
            pltpu.SemaphoreType.DMA((SLOTS,)),
            pltpu.SemaphoreType.DMA((4,)),
        ],
        compiler_params=pltpu.CompilerParams(vmem_limit_bytes=32 << 20),
        cost_estimate=pl.CostEstimate(
            flops=4 * doc_count * tok_count * width * rank,
            bytes_accessed=4 * doc_count * tok_count * width,
            transcendentals=0,
        ),
        name="partials",
    )(*map(in_hbm, (doc_lengths, inputs, out_grads, in_proj, out_proj, out_factor)))


def score_kernel(own, other, factor, index, out, applied, precond):
    owners, docs, owner_rows = out.shape
    part_docs, owned, rank = own[0].shape
    block = SCORED * owner_rows
    rows = part_docs * owned
    rep = lax.axis_index("rep")
    split = halves(factor[...])
    for pieces, place in ((own, rep), (other, 1 - rep)):
        total = sum(piece[...].astype(F32) for piece in pieces).reshape(rows, rank)
        total = dot3(halves(total), split)
        for lane in range(applied.shape[0]):
            applied[lane, pl.ds(pl.multiple_of(place * rows, rows), rows), :] = total[
                :, lane * LANES : (lane + 1) * LANES
            ]
    for o in range(owned):
        for lane in range(applied.shape[0]):
            start = o * rank + lane * LANES
            column = applied[lane, pl.ds(o, docs, stride=owned), :]
            precond[:, start : start + LANES] = column.astype(BF16)

    def one(k, carry):
        span = pl.ds(pl.multiple_of(k * block, block), block)
        scores = lax.dot_general(
            precond[...], index[span, :], (((1,), (1,)), ((), ())), preferred_element_type=F32
        )
        for j in range(SCORED):
            out[k * SCORED + j] = scores[:, j * owner_rows : (j + 1) * owner_rows]
        return carry

    lax.fori_loop(0, owners // SCORED, one, 0)


def score(own, other, in_factor, index_rows, owner_count):
    part_docs, owned, rank = own[0].shape
    docs = 2 * part_docs
    rows, features = index_rows.shape
    count = len(own)

    def kernel(*refs):
        score_kernel(refs[:count], refs[count : 2 * count], *refs[2 * count :])

    vmem = pl.BlockSpec(memory_space=pltpu.VMEM)
    return pl.pallas_call(
        kernel,
        out_shape=jax.ShapeDtypeStruct((owner_count, docs, rows // owner_count), F32),
        in_specs=[vmem] * (2 * count + 2),
        out_specs=vmem,
        scratch_shapes=[pltpu.VMEM((rank // LANES, docs * owned, LANES), F32), pltpu.VMEM((docs, features), BF16)],
        compiler_params=pltpu.CompilerParams(vmem_limit_bytes=8 << 20),
        cost_estimate=pl.CostEstimate(
            flops=2 * docs * rows * features, bytes_accessed=0, transcendentals=0
        ),
        name="score",
    )(*own, *other, in_factor, index_rows)


def to_partner(value, owner_count, offset):
    return lax.ppermute(value, OWNERS, [(i, i ^ offset) for i in range(owner_count)])


def fast(inputs, out_grads, doc_lengths, in_proj, out_proj, in_factor, out_factor, index_rows):
    owner_count = lax.axis_size(OWNERS)
    first, second = groups()
    pieces = partials(
        inputs, out_grads, doc_lengths, in_proj, out_proj, out_factor, first, second
    )
    got = [to_partner(pieces[i], owner_count, first[i]) for i in (2, 1, 3)] + [pieces[0]]
    sums = sum(g.astype(F32) for g in got).astype(BF16)
    rel = lax.optimization_barrier([sums[j] for j in range(len(second))])
    got = {
        second[j]: to_partner(rel[j], owner_count, second[j]) for j in range(1, len(second))
    }
    got[0] = rel[0]
    own = [got[b] for b in second if b % 2 == 0]
    other = [got[b] for b in second if b % 2 == 1]
    scores = score(own, other, in_factor, index_rows, owner_count)
    mine = lax.all_to_all(scores, OWNERS, split_axis=0, concat_axis=0, tiled=True)
    return jnp.sum(mine, axis=0).T


def plain(inputs, out_grads, doc_lengths, in_proj, out_proj, in_factor, out_factor, index_rows):
    doc_count, tok_count, model_width = inputs.shape
    rank_size = in_proj.shape[1]
    part_size = lax.axis_size(("seq", "sub"))
    rep_size = lax.axis_size("rep")
    owner_count = part_size * rep_size
    offset = lax.axis_index(("seq", "sub")) * tok_count
    positions = offset + jnp.arange(tok_count, dtype=jnp.int32)
    live = positions[None, :] < doc_lengths[:, None]
    in_rows = dot(inputs.reshape(-1, model_width), in_proj).astype(BF16)
    out_rows = dot(out_grads.reshape(-1, model_width), out_proj).astype(BF16)
    in_rows = in_rows.reshape(doc_count, tok_count, rank_size)
    out_rows = out_rows.reshape(doc_count, tok_count, rank_size)
    out_rows = jnp.where(live[:, :, None], out_rows, jnp.zeros_like(out_rows))
    grad = jnp.einsum("dto,dti->doi", out_rows, in_rows, preferred_element_type=F32)
    left = jnp.einsum("po,doi->dpi", out_factor, grad, precision=HI)
    part = jnp.einsum("dpi,iq->dpq", left, in_factor, precision=HI).astype(BF16)
    part = part.reshape(doc_count, owner_count, rank_size // owner_count, rank_size)
    part = part.transpose(1, 0, 2, 3)
    got = lax.all_to_all(part, OWNERS, split_axis=0, concat_axis=0, tiled=True)
    got = got.reshape(part_size, rep_size * doc_count, -1)
    precond = jnp.sum(got.astype(F32), axis=0).astype(BF16)
    scores = lax.dot_general(
        precond, index_rows, (((1,), (1,)), ((), ())), preferred_element_type=F32
    )
    rows = scores.shape[1] // owner_count
    scores = scores.reshape(-1, owner_count, rows).transpose(1, 0, 2)
    mine = lax.all_to_all(scores, OWNERS, split_axis=0, concat_axis=0, tiled=True)
    return jnp.sum(mine, axis=0).T


def on_device(*args):
    owner_count = lax.axis_size(OWNERS)
    rank_size = args[3].shape[1]
    sizes = tuple(lax.axis_size(axis) for axis in OWNERS)
    docs = sizes[2] * args[0].shape[0]
    if sizes == (4, 2, 2) and docs == 8 and rank_size % (16 * owner_count) == 0:
        return fast(*args)
    return plain(*args)


def solution(mesh):
    in_specs = (
        P(("grp", "rep"), ("seq", "sub"), None),
        P(("grp", "rep"), ("seq", "sub"), None),
        P(("grp", "rep")),
        P(),
        P(),
        P(),
        P(),
        P("grp", ("seq", "sub", "rep")),
    )
    out_specs = P(("grp", "seq", "sub", "rep"), None)
    return jax.shard_map(
        on_device, mesh=mesh, in_specs=in_specs, out_specs=out_specs, check_vma=False
    )
```

```python
import functools

import jax
import jax.numpy as jnp
from jax import lax
from jax.experimental import pallas as pl
from jax.experimental.pallas import tpu as pltpu
from jax.sharding import PartitionSpec as P

HI = lax.Precision.HIGHEST
BF16 = jnp.bfloat16
F32 = jnp.float32
OWNERS = ("seq", "sub", "rep")
FLIGHT = 3
SLOTS = 4
LANES = 128
SUBLANES = 16


def halves(a):
    high = a.astype(BF16)
    return high, (a - high.astype(F32)).astype(BF16)


def dot(a, b):
    return jnp.dot(a, b, preferred_element_type=F32)


def dot3(a, b):
    return dot(a[0], b[0]) + (dot(a[0], b[1]) + dot(a[1], b[0]))


def in_hbm(array):
    return pltpu.with_memory_space_constraint(array, pltpu.HBM)


def spans(bits):
    found = [0]
    for bit in bits:
        found = found + [bit ^ f for f in found]
    return found


def groups(owner_count):
    bits = [1 << i for i in range(owner_count.bit_length() - 1)]
    return spans(bits[1:3]), spans(bits[3:] + bits[:1])


def partial_kernel(first, second, lengths_hbm, x_hbm, g_hbm, pin_hbm, pout_hbm, factor_hbm, *rest):
    outs, rest = rest[: len(first)], rest[len(first) :]
    proj, held, kept_in, kept_out, grads, whole, factor, split, lengths, sems, once = rest
    slots, tok_count, _ = held.shape
    doc_count = x_hbm.shape[0]
    owned = outs[0].shape[2]
    part = lax.axis_index("seq") * lax.axis_size("sub") + lax.axis_index("sub")
    me = part * lax.axis_size("rep") + lax.axis_index("rep")
    base = part * tok_count
    items = 2 * doc_count

    def load(item, side):
        slot = lax.rem(item, slots)
        return pltpu.make_async_copy((x_hbm, g_hbm)[side].at[item // 2], held.at[slot], sems.at[slot])

    project = [
        pltpu.make_async_copy((pin_hbm, pout_hbm)[s], proj.at[s], once.at[s]) for s in range(2)
    ]
    small = [
        pltpu.make_async_copy(factor_hbm, factor, once.at[2]),
        pltpu.make_async_copy(lengths_hbm, lengths, once.at[3]),
    ]
    project[0].start()
    load(0, 0).start()
    load(1, 1).start()
    project[1].start()
    load(2, 0).start()
    for copy in small:
        copy.start()
    project[0].wait()

    def scatter(doc, values):
        whole[...] = values
        for i, a in enumerate(first):
            for j, b in enumerate(second):
                start = pl.multiple_of((me ^ (a ^ b)) * owned, owned)
                outs[i][j, doc] = whole[pl.ds(start, owned), :].astype(BF16)

    def gradient(doc):
        return lax.dot_general(
            kept_out[...],
            kept_in[lax.rem(doc, 2)],
            (((0,), (0,)), ((), ())),
            preferred_element_type=F32,
        )

    def finish(doc):
        scatter(doc, dot3((split[0], split[1]), halves(gradient(doc))), 0)

    def one(item, carry):
        doc = item // 2
        side = lax.rem(item, 2)

        @pl.when(item == 1)
        def _():
            project[1].wait()
            for copy in small:
                copy.wait()
            split[0], split[1] = halves(factor[...])

        load(item, 0).wait()

        @pl.when((item + FLIGHT < items) & (side == 1))
        def _():
            load(item + FLIGHT, 0).start()

        @pl.when((item + FLIGHT < items) & (side == 0))
        def _():
            load(item + FLIGHT, 1).start()

        @pl.when(side == 0)
        def _():
            rows = dot(held[lax.rem(item, slots)], proj[0])
            kept_in[lax.rem(doc, 2)] = rows.astype(BF16)
            grads[jnp.maximum(doc - 1, 0)] = gradient(jnp.maximum(doc - 1, 0))

        @pl.when(side == 1)
        def _():
            rows = dot(held[lax.rem(item, slots)], proj[1])
            position = base + lax.broadcasted_iota(jnp.int32, rows.shape, 0)
            kept_out[...] = jnp.where(position < lengths[doc], rows, 0.0).astype(BF16)

        return carry

    lax.fori_loop(0, items, one, 0)
    grads[doc_count - 1] = gradient(doc_count - 1)
    for doc in range(doc_count):
        scatter(doc, dot3((split[0], split[1]), halves(grads[doc])))


def partials(inputs, out_grads, doc_lengths, in_proj, out_proj, out_factor, first, second):
    doc_count, tok_count, width = inputs.shape
    rank = in_proj.shape[1]
    owned = rank // (len(first) * len(second))
    hbm = pl.BlockSpec(memory_space=pltpu.HBM)
    vmem = pl.BlockSpec(memory_space=pltpu.VMEM)
    return pl.pallas_call(
        functools.partial(partial_kernel, first, second),
        out_shape=[jax.ShapeDtypeStruct((len(second), doc_count, owned, rank), BF16)] * len(first),
        in_specs=[hbm] * 6,
        out_specs=[vmem] * len(first),
        scratch_shapes=[
            pltpu.VMEM((2, width, rank), BF16),
            pltpu.VMEM((SLOTS, tok_count, width), BF16),
            pltpu.VMEM((2, tok_count, rank), BF16),
            pltpu.VMEM((tok_count, rank), BF16),
            pltpu.VMEM((doc_count, rank, rank), F32),
            pltpu.VMEM((rank, rank), F32),
            pltpu.VMEM((rank, rank), F32),
            pltpu.VMEM((2, rank, rank), BF16),
            pltpu.SMEM((doc_count,), jnp.int32),
            pltpu.SemaphoreType.DMA((SLOTS,)),
            pltpu.SemaphoreType.DMA((4,)),
        ],
        compiler_params=pltpu.CompilerParams(vmem_limit_bytes=32 << 20),
        cost_estimate=pl.CostEstimate(
            flops=4 * doc_count * tok_count * width * rank,
            bytes_accessed=4 * doc_count * tok_count * width,
            transcendentals=0,
        ),
        name="partials",
    )(*map(in_hbm, (doc_lengths, inputs, out_grads, in_proj, out_proj, out_factor)))


def score_kernel(own, other, factor, index, out, applied, precond):
    owners, docs, owner_rows = out.shape
    part_docs, owned, rank = own[0].shape
    rows = part_docs * owned
    rep = lax.axis_index("rep")
    split = halves(factor[...])
    for pieces, place in ((own, rep), (other, 1 - rep)):
        total = sum(piece[...].astype(F32) for piece in pieces).reshape(rows, rank)
        total = dot3(halves(total), split)
        for lane in range(applied.shape[0]):
            applied[lane, pl.ds(pl.multiple_of(place * rows, rows), rows), :] = total[
                :, lane * LANES : (lane + 1) * LANES
            ]
    for o in range(owned):
        for lane in range(applied.shape[0]):
            start = o * rank + lane * LANES
            column = applied[lane, pl.ds(o, docs, stride=owned), :]
            precond[:, start : start + LANES] = column.astype(BF16)

    scores = lax.dot_general(
        precond[...], index[...], (((1,), (1,)), ((), ())), preferred_element_type=F32
    )
    for k in range(owners):
        out[k] = scores[:, k * owner_rows : (k + 1) * owner_rows]


def score(own, other, in_factor, index_rows, owner_count):
    part_docs, owned, rank = own[0].shape
    docs = 2 * part_docs
    rows, features = index_rows.shape
    count = len(own)

    def kernel(*refs):
        score_kernel(refs[:count], refs[count : 2 * count], *refs[2 * count :])

    vmem = pl.BlockSpec(memory_space=pltpu.VMEM)
    return pl.pallas_call(
        kernel,
        out_shape=jax.ShapeDtypeStruct((owner_count, docs, rows // owner_count), F32),
        in_specs=[vmem] * (2 * count + 2),
        out_specs=vmem,
        scratch_shapes=[pltpu.VMEM((rank // LANES, docs * owned, LANES), F32), pltpu.VMEM((docs, features), BF16)],
        compiler_params=pltpu.CompilerParams(vmem_limit_bytes=8 << 20),
        cost_estimate=pl.CostEstimate(
            flops=2 * docs * rows * features, bytes_accessed=0, transcendentals=0
        ),
        name="score",
    )(*own, *other, in_factor, index_rows)


def to_partner(value, owner_count, offset):
    return lax.ppermute(value, OWNERS, [(i, i ^ offset) for i in range(owner_count)])


def fast(inputs, out_grads, doc_lengths, in_proj, out_proj, in_factor, out_factor, index_rows):
    owner_count = lax.axis_size(OWNERS)
    first, second = groups(owner_count)
    pieces = partials(
        inputs, out_grads, doc_lengths, in_proj, out_proj, out_factor, first, second
    )
    got = [to_partner(pieces[i], owner_count, first[i]) for i in (2, 1, 3)] + [pieces[0]]
    sums = sum(g.astype(F32) for g in got).astype(BF16)
    rel = lax.optimization_barrier([sums[j] for j in range(len(second))])
    got = {
        second[j]: to_partner(rel[j], owner_count, second[j]) for j in range(1, len(second))
    }
    got[0] = rel[0]
    own = [got[b] for b in second if b % 2 == 0]
    other = [got[b] for b in second if b % 2 == 1]
    scores = score(own, other, in_factor, index_rows, owner_count)
    mine = lax.all_to_all(scores, OWNERS, split_axis=0, concat_axis=0, tiled=True)
    return jnp.sum(mine, axis=0).T


def plain(inputs, out_grads, doc_lengths, in_proj, out_proj, in_factor, out_factor, index_rows):
    doc_count, tok_count, model_width = inputs.shape
    rank_size = in_proj.shape[1]
    part_size = lax.axis_size(("seq", "sub"))
    rep_size = lax.axis_size("rep")
    owner_count = part_size * rep_size
    offset = lax.axis_index(("seq", "sub")) * tok_count
    positions = offset + jnp.arange(tok_count, dtype=jnp.int32)
    live = positions[None, :] < doc_lengths[:, None]
    in_rows = dot(inputs.reshape(-1, model_width), in_proj).astype(BF16)
    out_rows = dot(out_grads.reshape(-1, model_width), out_proj).astype(BF16)
    in_rows = in_rows.reshape(doc_count, tok_count, rank_size)
    out_rows = out_rows.reshape(doc_count, tok_count, rank_size)
    out_rows = jnp.where(live[:, :, None], out_rows, jnp.zeros_like(out_rows))
    grad = jnp.einsum("dto,dti->doi", out_rows, in_rows, preferred_element_type=F32)
    left = jnp.einsum("po,doi->dpi", out_factor, grad, precision=HI)
    part = jnp.einsum("dpi,iq->dpq", left, in_factor, precision=HI).astype(BF16)
    part = part.reshape(doc_count, owner_count, rank_size // owner_count, rank_size)
    part = part.transpose(1, 0, 2, 3)
    got = lax.all_to_all(part, OWNERS, split_axis=0, concat_axis=0, tiled=True)
    got = got.reshape(part_size, rep_size * doc_count, -1)
    precond = jnp.sum(got.astype(F32), axis=0).astype(BF16)
    scores = lax.dot_general(
        precond, index_rows, (((1,), (1,)), ((), ())), preferred_element_type=F32
    )
    rows = scores.shape[1] // owner_count
    scores = scores.reshape(-1, owner_count, rows).transpose(1, 0, 2)
    mine = lax.all_to_all(scores, OWNERS, split_axis=0, concat_axis=0, tiled=True)
    return jnp.sum(mine, axis=0).T


def on_device(*args):
    owner_count = lax.axis_size(OWNERS)
    rank_size = args[3].shape[1]
    paired = lax.axis_size("rep") == 2 and owner_count & (owner_count - 1) == 0
    if paired and owner_count > 4 and rank_size % (SUBLANES * owner_count) == 0:
        return fast(*args)
    return plain(*args)


def solution(mesh):
    in_specs = (
        P(("grp", "rep"), ("seq", "sub"), None),
        P(("grp", "rep"), ("seq", "sub"), None),
        P(("grp", "rep")),
        P(),
        P(),
        P(),
        P(),
        P("grp", ("seq", "sub", "rep")),
    )
    out_specs = P(("grp", "seq", "sub", "rep"), None)
    return jax.shard_map(
        on_device, mesh=mesh, in_specs=in_specs, out_specs=out_specs, check_vma=False
    )
```

```python
import functools

import jax
import jax.numpy as jnp
from jax import lax
from jax.experimental import pallas as pl
from jax.experimental.pallas import tpu as pltpu
from jax.sharding import PartitionSpec as P

HI = lax.Precision.HIGHEST
BF16 = jnp.bfloat16
F32 = jnp.float32
OWNERS = ("seq", "sub", "rep")
FLIGHT = 3
SLOTS = 4
LANES = 128
SUBLANES = 16


def halves(a):
    high = a.astype(BF16)
    return high, (a - high.astype(F32)).astype(BF16)


def dot(a, b):
    return jnp.dot(a, b, preferred_element_type=F32)


def dot3(a, b):
    return dot(a[0], b[0]) + (dot(a[0], b[1]) + dot(a[1], b[0]))


def in_hbm(array):
    return pltpu.with_memory_space_constraint(array, pltpu.HBM)


def spans(bits):
    found = [0]
    for bit in bits:
        found = found + [bit ^ f for f in found]
    return found


def groups(owner_count):
    bits = [1 << i for i in range(owner_count.bit_length() - 1)]
    return spans(bits[1:3]), spans(bits[3:] + bits[:1])


def partial_kernel(first, second, lengths_hbm, x_hbm, g_hbm, pin_hbm, pout_hbm, factor_hbm, *rest):
    outs, rest = rest[: len(first)], rest[len(first) :]
    proj, held, kept_in, kept_out, grads, whole, factor, split, lengths, sems, once = rest
    slots, tok_count, _ = held.shape
    doc_count = x_hbm.shape[0]
    owned = outs[0].shape[2]
    part = lax.axis_index("seq") * lax.axis_size("sub") + lax.axis_index("sub")
    me = part * lax.axis_size("rep") + lax.axis_index("rep")
    base = part * tok_count
    items = 2 * doc_count

    def load(item, side):
        slot = lax.rem(item, slots)
        return pltpu.make_async_copy((x_hbm, g_hbm)[side].at[item // 2], held.at[slot], sems.at[slot])

    project = [
        pltpu.make_async_copy((pin_hbm, pout_hbm)[s], proj.at[s], once.at[s]) for s in range(2)
    ]
    small = [
        pltpu.make_async_copy(factor_hbm, factor, once.at[2]),
        pltpu.make_async_copy(lengths_hbm, lengths, once.at[3]),
    ]
    project[0].start()
    load(0, 0).start()
    load(1, 1).start()
    project[1].start()
    load(2, 0).start()
    for copy in small:
        copy.start()
    project[0].wait()

    def scatter(doc, values):
        whole[...] = values
        for i, a in enumerate(first):
            for j, b in enumerate(second):
                start = pl.multiple_of((me ^ (a ^ b)) * owned, owned)
                outs[i][j, doc] = whole[pl.ds(start, owned), :].astype(BF16)

    def gradient(doc):
        return lax.dot_general(
            kept_out[...],
            kept_in[lax.rem(doc, 2)],
            (((0,), (0,)), ((), ())),
            preferred_element_type=F32,
        )

    def finish(doc):
        scatter(doc, dot3((split[0], split[1]), halves(gradient(doc))), 0)

    def one(item, carry):
        doc = item // 2
        side = lax.rem(item, 2)

        @pl.when(item == 1)
        def _():
            project[1].wait()
            for copy in small:
                copy.wait()
            split[0], split[1] = halves(factor[...])

        load(item, 0).wait()

        @pl.when((item + FLIGHT < items) & (side == 1))
        def _():
            load(item + FLIGHT, 0).start()

        @pl.when((item + FLIGHT < items) & (side == 0))
        def _():
            load(item + FLIGHT, 1).start()

        @pl.when(side == 0)
        def _():
            rows = dot(held[lax.rem(item, slots)], proj[0])
            kept_in[lax.rem(doc, 2)] = rows.astype(BF16)
            grads[jnp.maximum(doc - 1, 0)] = gradient(jnp.maximum(doc - 1, 0))

        @pl.when(side == 1)
        def _():
            rows = dot(held[lax.rem(item, slots)], proj[1])
            position = base + lax.broadcasted_iota(jnp.int32, rows.shape, 0)
            kept_out[...] = jnp.where(position < lengths[doc], rows, 0.0).astype(BF16)

        return carry

    lax.fori_loop(0, items, one, 0)
    grads[doc_count - 1] = gradient(doc_count - 1)
    for doc in range(doc_count):
        scatter(doc, dot3((split[0], split[1]), halves(grads[doc])))


def partials(inputs, out_grads, doc_lengths, in_proj, out_proj, out_factor, first, second):
    doc_count, tok_count, width = inputs.shape
    rank = in_proj.shape[1]
    owned = rank // (len(first) * len(second))
    hbm = pl.BlockSpec(memory_space=pltpu.HBM)
    vmem = pl.BlockSpec(memory_space=pltpu.VMEM)
    return pl.pallas_call(
        functools.partial(partial_kernel, first, second),
        out_shape=[jax.ShapeDtypeStruct((len(second), doc_count, owned, rank), BF16)] * len(first),
        in_specs=[hbm] * 6,
        out_specs=[vmem] * len(first),
        scratch_shapes=[
            pltpu.VMEM((2, width, rank), BF16),
            pltpu.VMEM((SLOTS, tok_count, width), BF16),
            pltpu.VMEM((2, tok_count, rank), BF16),
            pltpu.VMEM((tok_count, rank), BF16),
            pltpu.VMEM((doc_count, rank, rank), F32),
            pltpu.VMEM((rank, rank), F32),
            pltpu.VMEM((rank, rank), F32),
            pltpu.VMEM((2, rank, rank), BF16),
            pltpu.SMEM((doc_count,), jnp.int32),
            pltpu.SemaphoreType.DMA((SLOTS,)),
            pltpu.SemaphoreType.DMA((4,)),
        ],
        compiler_params=pltpu.CompilerParams(vmem_limit_bytes=32 << 20),
        cost_estimate=pl.CostEstimate(
            flops=4 * doc_count * tok_count * width * rank,
            bytes_accessed=4 * doc_count * tok_count * width,
            transcendentals=0,
        ),
        name="partials",
    )(*map(in_hbm, (doc_lengths, inputs, out_grads, in_proj, out_proj, out_factor)))


def score_kernel(own, other, factor, index, out, applied, precond):
    owners, docs, owner_rows = out.shape
    part_docs, owned, rank = own[0].shape
    rows = part_docs * owned
    rep = lax.axis_index("rep")
    split = halves(factor[...])
    for pieces, place in ((own, rep), (other, 1 - rep)):
        total = sum(piece[...].astype(F32) for piece in pieces).reshape(rows, rank)
        total = dot3(halves(total), split)
        for lane in range(applied.shape[0]):
            applied[lane, pl.ds(pl.multiple_of(place * rows, rows), rows), :] = total[
                :, lane * LANES : (lane + 1) * LANES
            ]
    for o in range(owned):
        for lane in range(applied.shape[0]):
            start = o * rank + lane * LANES
            column = applied[lane, pl.ds(o, docs, stride=owned), :]
            precond[:, start : start + LANES] = column.astype(BF16)

    scores = lax.dot_general(
        precond[...], index[...], (((1,), (1,)), ((), ())), preferred_element_type=F32
    )
    for k in range(owners):
        out[k] = scores[:, k * owner_rows : (k + 1) * owner_rows]


def score(own, other, in_factor, index_rows, owner_count):
    part_docs, owned, rank = own[0].shape
    docs = 2 * part_docs
    rows, features = index_rows.shape
    count = len(own)

    def kernel(*refs):
        score_kernel(refs[:count], refs[count : 2 * count], *refs[2 * count :])

    vmem = pl.BlockSpec(memory_space=pltpu.VMEM)
    return pl.pallas_call(
        kernel,
        out_shape=jax.ShapeDtypeStruct((owner_count, docs, rows // owner_count), F32),
        in_specs=[vmem] * (2 * count + 2),
        out_specs=vmem,
        scratch_shapes=[pltpu.VMEM((rank // LANES, docs * owned, LANES), F32), pltpu.VMEM((docs, features), BF16)],
        compiler_params=pltpu.CompilerParams(vmem_limit_bytes=8 << 20),
        cost_estimate=pl.CostEstimate(
            flops=2 * docs * rows * features, bytes_accessed=0, transcendentals=0
        ),
        name="score",
    )(*own, *other, in_factor, index_rows)


def to_partner(value, owner_count, offset):
    return lax.ppermute(value, OWNERS, [(i, i ^ offset) for i in range(owner_count)])


def fast(inputs, out_grads, doc_lengths, in_proj, out_proj, in_factor, out_factor, index_rows):
    owner_count = lax.axis_size(OWNERS)
    first, second = groups(owner_count)
    pieces = partials(
        inputs, out_grads, doc_lengths, in_proj, out_proj, out_factor, first, second
    )
    got = [to_partner(pieces[i], owner_count, first[i]) for i in (2, 1, 3)] + [pieces[0]]
    rel = [sum(g[j].astype(F32) for g in got).astype(BF16) for j in range(len(second))]
    got = {
        second[j]: to_partner(rel[j], owner_count, second[j]) for j in range(1, len(second))
    }
    got[0] = rel[0]
    own = [got[b] for b in second if b % 2 == 0]
    other = [got[b] for b in second if b % 2 == 1]
    scores = score(own, other, in_factor, index_rows, owner_count)
    mine = lax.all_to_all(scores, OWNERS, split_axis=0, concat_axis=0, tiled=True)
    return jnp.sum(mine, axis=0).T


def plain(inputs, out_grads, doc_lengths, in_proj, out_proj, in_factor, out_factor, index_rows):
    doc_count, tok_count, model_width = inputs.shape
    rank_size = in_proj.shape[1]
    part_size = lax.axis_size(("seq", "sub"))
    rep_size = lax.axis_size("rep")
    owner_count = part_size * rep_size
    offset = lax.axis_index(("seq", "sub")) * tok_count
    positions = offset + jnp.arange(tok_count, dtype=jnp.int32)
    live = positions[None, :] < doc_lengths[:, None]
    in_rows = dot(inputs.reshape(-1, model_width), in_proj).astype(BF16)
    out_rows = dot(out_grads.reshape(-1, model_width), out_proj).astype(BF16)
    in_rows = in_rows.reshape(doc_count, tok_count, rank_size)
    out_rows = out_rows.reshape(doc_count, tok_count, rank_size)
    out_rows = jnp.where(live[:, :, None], out_rows, jnp.zeros_like(out_rows))
    grad = jnp.einsum("dto,dti->doi", out_rows, in_rows, preferred_element_type=F32)
    left = jnp.einsum("po,doi->dpi", out_factor, grad, precision=HI)
    part = jnp.einsum("dpi,iq->dpq", left, in_factor, precision=HI).astype(BF16)
    part = part.reshape(doc_count, owner_count, rank_size // owner_count, rank_size)
    part = part.transpose(1, 0, 2, 3)
    got = lax.all_to_all(part, OWNERS, split_axis=0, concat_axis=0, tiled=True)
    got = got.reshape(part_size, rep_size * doc_count, -1)
    precond = jnp.sum(got.astype(F32), axis=0).astype(BF16)
    scores = lax.dot_general(
        precond, index_rows, (((1,), (1,)), ((), ())), preferred_element_type=F32
    )
    rows = scores.shape[1] // owner_count
    scores = scores.reshape(-1, owner_count, rows).transpose(1, 0, 2)
    mine = lax.all_to_all(scores, OWNERS, split_axis=0, concat_axis=0, tiled=True)
    return jnp.sum(mine, axis=0).T


def on_device(*args):
    owner_count = lax.axis_size(OWNERS)
    rank_size = args[3].shape[1]
    paired = lax.axis_size("rep") == 2 and owner_count & (owner_count - 1) == 0
    if paired and owner_count > 4 and rank_size % (SUBLANES * owner_count) == 0:
        return fast(*args)
    return plain(*args)


def solution(mesh):
    in_specs = (
        P(("grp", "rep"), ("seq", "sub"), None),
        P(("grp", "rep"), ("seq", "sub"), None),
        P(("grp", "rep")),
        P(),
        P(),
        P(),
        P(),
        P("grp", ("seq", "sub", "rep")),
    )
    out_specs = P(("grp", "seq", "sub", "rep"), None)
    return jax.shard_map(
        on_device, mesh=mesh, in_specs=in_specs, out_specs=out_specs, check_vma=False
    )
```
